32 devices in a mesh: row: 4 (over y, x), col: 8 (over z, core).
Axes of the slice: x: 2, y: 2, z: 4, core: 2. Of those that a mesh axis runs over, the one named last changes fastest.
Arguments:
- pixels: float32 [3, 192, 256], P(None, 'row', 'col'), may hold values from -6 to 6
- stem_weight: bfloat16 [64, 3, 4, 4], replicated, may hold values from -0.875 to 0.875
- first_weight: bfloat16 [64, 64, 3, 3], replicated, may hold values from -0.25 to 0.25
- second_weight: bfloat16 [64, 64, 3, 3], replicated, may hold values from -0.25 to 0.25
- entry_weight: bfloat16 [256, 64, 3, 3], P('col'), may hold values from -0.25 to 0.25
- final_weight: bfloat16 [256, 256, 3, 3], P('col'), may hold values from -0.125 to 0.125
- upstream: bfloat16 [256, 96, 128], P('col', 'row'), may hold values from -6 to 6
Outputs:
- stem_grad: float32 [64, 3, 4, 4], replicated
- first_grad: float32 [64, 64, 3, 3], replicated
- second_grad: float32 [64, 64, 3, 3], replicated
- entry_grad: float32 [256, 64, 3, 3], P('col')
- final_grad: float32 [256, 256, 3, 3], P('col')
The draws below stay inside these ranges and needn't reach their ends.
All inputs are finite; a program needn't handle non-finite values.
Results may differ from the reference program's by a relative error of at most 0.023.
Values may be sent and summed in bfloat16 or wider, within the bound.
A program may use at most 64 MiB of HBM per device.

```python
import math
import jax
import jax.numpy as jnp
from jax import lax

C_IN = 3
F = 64
G = 256
HH = 96
WW = 128
H = 192
W = 256
G_DEV = 32
N_COL = 8


def block_levels(key, dims, pieces, low, high):
    def one(axis_at, shards_of):
        draws = jax.random.uniform(jax.random.fold_in(jax.random.fold_in(key, 6), axis_at), (shards_of,), jnp.float32, low / len(pieces), high / len(pieces))
        return jnp.repeat(jnp.exp(draws), dims[axis_at] // shards_of).reshape((-1,) + (1,) * (len(dims) - axis_at - 1))

    level = one(*pieces[0])
    for cut in pieces[1:]:
        level = level * one(*cut)
    return level


def scatter_about(own_key, extent, scale, reach, shards=(), kind=jnp.bfloat16):
    array = scale * jax.random.normal(own_key, extent, jnp.float32)
    if shards:
        array = array * block_levels(own_key, extent, shards, -0.22, 0.18)
    return jnp.clip(array, -reach, reach).astype(kind)


def setup_inputs(seed: int = 0) -> dict:
    streams_of = jax.random.split(jax.random.key(seed), 8)
    return {
        "pixels": scatter_about(streams_of[0], (C_IN, H, W), 1.0, 6.0, ((1, 4), (2, 8)), jnp.float32),
        "stem_weight": scatter_about(streams_of[1], (F, C_IN, 4, 4), (C_IN * 16) ** -0.5, 0.875),
        "first_weight": scatter_about(streams_of[2], (F, F, 3, 3), (F * 9) ** -0.5, 0.25),
        "second_weight": scatter_about(streams_of[3], (F, F, 3, 3), (F * 9) ** -0.5, 0.25),
        "entry_weight": scatter_about(streams_of[4], (G, F, 3, 3), (F * 9) ** -0.5, 0.25, ((0, 8),)),
        "final_weight": scatter_about(streams_of[5], (G, G, 3, 3), (G * 9) ** -0.5, 0.125, ((0, 8),)),
        "upstream": scatter_about(streams_of[6], (G, HH, WW), 1.0, 6.0, ((0, 8), (1, 4))),
    }


def conv_valid(field, kernel, stride):
    return lax.conv_general_dilated(field[None], kernel, (stride, stride), 'VALID', dimension_numbers=('NCHW', 'OIHW', 'NCHW'), preferred_element_type=jnp.float32)[0]

def weight_grad(padded, upstream, stride):
    result = lax.conv_general_dilated(padded[:, None], upstream[:, None], (1, 1), 'VALID', rhs_dilation=(stride, stride), dimension_numbers=('NCHW', 'OIHW', 'NCHW'), preferred_element_type=jnp.float32)
    return result.transpose(1, 0, 2, 3)

def back_kernel(kernel):
    return jnp.flip(kernel, (2, 3)).transpose(1, 0, 2, 3)

def silu_slope(values):
    logistic = jax.nn.sigmoid(values)
    return logistic * (1.0 + values * (1.0 - logistic))

def border(field):
    return jnp.pad(field, ((0, 0), (1, 1), (1, 1)))

def reference(pixels, stem_weight, first_weight, second_weight, entry_weight, final_weight, upstream):
    norm_scale = 1.0 / math.sqrt(HH * WW)
    inputs = pixels.astype(jnp.bfloat16)
    padded_in = border(inputs)
    stem_pre = conv_valid(padded_in, stem_weight, 2)
    stem_act = border(jax.nn.silu(stem_pre).astype(jnp.bfloat16))
    first_pre = conv_valid(stem_act, first_weight, 1)
    first_act = border(jax.nn.silu(first_pre).astype(jnp.bfloat16))
    second_pre = conv_valid(first_act, second_weight, 1)
    second_act = border(jax.nn.silu(second_pre).astype(jnp.bfloat16))
    entry_pre = conv_valid(second_act, entry_weight, 1)
    entry_act = border(jax.nn.silu(entry_pre).astype(jnp.bfloat16))
    final_grad = weight_grad(entry_act, upstream, 1)
    groups_kernel = final_weight.reshape(N_COL, G_DEV, G, 3, 3)
    groups_up = border(upstream).reshape(N_COL, G_DEV, HH + 2, WW + 2)

    def add_group(running, member):
        partial_value = conv_valid(member[1], back_kernel(member[0]), 1).astype(jnp.bfloat16)
        partial_value = lax.optimization_barrier(partial_value)
        return (running + partial_value.astype(jnp.float32), None)
    entry_back, ignored = lax.scan(add_group, jnp.zeros((G, HH, WW), jnp.float32), (groups_kernel, groups_up))
    entry_delta = (entry_back * silu_slope(entry_pre)).astype(jnp.bfloat16)
    entry_grad = weight_grad(second_act, entry_delta, 1)
    second_back = conv_valid(border(entry_delta), back_kernel(entry_weight), 1)
    second_delta = (second_back * silu_slope(second_pre)).astype(jnp.bfloat16)
    second_grad = weight_grad(first_act, second_delta, 1)
    first_back = conv_valid(border(second_delta), back_kernel(second_weight), 1)
    first_delta = (first_back * silu_slope(first_pre)).astype(jnp.bfloat16)
    first_grad = weight_grad(stem_act, first_delta, 1)
    stem_back = conv_valid(border(first_delta), back_kernel(first_weight), 1)
    stem_delta = (stem_back * silu_slope(stem_pre)).astype(jnp.bfloat16)
    stem_grad = weight_grad(padded_in, stem_delta, 2)
    return (stem_grad * norm_scale, first_grad * norm_scale, second_grad * norm_scale, entry_grad * norm_scale, final_grad * norm_scale)
```

```python
import functools
import math

import jax
import jax.numpy as jnp
from jax import lax
from jax.experimental import pallas as pl
from jax.experimental.pallas import tpu as pltpu
from jax.sharding import PartitionSpec as P

BF = jnp.bfloat16
F32 = jnp.float32


MESH = pl.DeviceIdType.MESH
VMEM = pl.BlockSpec(memory_space=pltpu.VMEM)
RIM = 16
UP_RIM = 4


def start_kernel(rows_of, cols_of, pix_ref, up_ref, pix_out, up_out, sends, pix_recv, rim_recv, up_recv, own_sems):
    row, col = lax.axis_index("row"), lax.axis_index("col")
    tall, up_rows = pix_ref.shape[0], up_ref.shape[0]
    barrier = pltpu.get_barrier_semaphore()
    not_first, not_last = row > 0, row < rows_of - 1

    for k in range(1, cols_of):
        peer = lax.rem(col + k, cols_of)
        pl.semaphore_signal(barrier, inc=1, device_id=(row, peer), device_id_type=MESH)
    for side, there in ((-1, not_first), (1, not_last)):

        @pl.when(there)
        def _():
            for k in range(cols_of):
                peer = lax.rem(col + k, cols_of)
                pl.semaphore_signal(
                    barrier, inc=1, device_id=(row + side, peer), device_id_type=MESH
                )

    bands = 1 + not_first.astype(jnp.int32) + not_last.astype(jnp.int32)
    pl.semaphore_wait(barrier, bands * cols_of - 1)

    def tile_copy(k):
        return pltpu.make_async_remote_copy(
            src_ref=pix_ref,
            dst_ref=pix_out.at[k, RIM : RIM + tall],
            send_sem=sends.at[0, k],
            recv_sem=pix_recv.at[k],
            device_id=(row, lax.rem(col + k, cols_of)),
            device_id_type=MESH,
        )

    def rim_copy(side, k):
        src = pix_ref.at[0:RIM] if side < 0 else pix_ref.at[tall - RIM : tall]
        dst = pix_out.at[k, RIM + tall : tall + 2 * RIM] if side < 0 else pix_out.at[k, 0:RIM]
        at = 0 if side < 0 else 1
        return pltpu.make_async_remote_copy(
            src_ref=src,
            dst_ref=dst,
            send_sem=sends.at[1 + at, k],
            recv_sem=rim_recv.at[at, k],
            device_id=(row + side, lax.rem(col + k, cols_of)),
            device_id_type=MESH,
        )

    def up_copy(side):
        src = up_ref.at[0:UP_RIM] if side < 0 else up_ref.at[up_rows - UP_RIM : up_rows]
        dst = up_out.at[UP_RIM + up_rows : up_rows + 2 * UP_RIM] if side < 0 else up_out.at[0:UP_RIM]
        at = 0 if side < 0 else 1
        return pltpu.make_async_remote_copy(
            src_ref=src,
            dst_ref=dst,
            send_sem=sends.at[3, at],
            recv_sem=up_recv.at[at],
            device_id=(row + side, col),
            device_id_type=MESH,
        )

    sides = ((-1, not_first), (1, not_last))
    for side, there in sides:

        @pl.when(there)
        def _():
            up_copy(side).start()
            for k in range(cols_of):
                rim_copy(side, k).start()

    for k in range(1, cols_of):
        tile_copy(k).start()
    own_pix = pltpu.make_async_copy(pix_ref, pix_out.at[0, RIM : RIM + tall], own_sems.at[0])
    own_up = pltpu.make_async_copy(up_ref, up_out.at[UP_RIM : UP_RIM + up_rows], own_sems.at[1])
    own_pix.start()
    own_up.start()

    @pl.when(row == 0)
    def _():
        for k in range(cols_of):
            pix_out[k, 0:RIM] = jnp.zeros((RIM, pix_ref.shape[1]), BF)
        up_out[0:UP_RIM] = jnp.zeros((UP_RIM,) + up_ref.shape[1:], BF)

    @pl.when(row == rows_of - 1)
    def _():
        for k in range(cols_of):
            pix_out[k, RIM + tall : tall + 2 * RIM] = jnp.zeros((RIM, pix_ref.shape[1]), BF)
        up_out[UP_RIM + up_rows : up_rows + 2 * UP_RIM] = jnp.zeros((UP_RIM,) + up_ref.shape[1:], BF)

    own_pix.wait()
    own_up.wait()
    for k in range(1, cols_of):
        tile_copy(k).wait()
    for side, there in sides:

        @pl.when(there)
        def _():
            up_copy(side).wait_send()
            for k in range(cols_of):
                rim_copy(side, k).wait_send()

        other = not_last if side < 0 else not_first

        @pl.when(other)
        def _():
            up_copy(side).wait_recv()
            for k in range(cols_of):
                rim_copy(side, k).wait_recv()


def start(pix, up):
    rows_of, cols_of = lax.axis_size("row"), lax.axis_size("col")
    return pl.pallas_call(
        functools.partial(start_kernel, rows_of, cols_of),
        out_shape=(
            jax.ShapeDtypeStruct((cols_of, pix.shape[0] + 2 * RIM, pix.shape[1]), BF),
            jax.ShapeDtypeStruct((up.shape[0] + 2 * UP_RIM,) + up.shape[1:], BF),
        ),
        in_specs=[VMEM] * 2,
        out_specs=(VMEM, VMEM),
        scratch_shapes=[
            pltpu.SemaphoreType.DMA((4, cols_of)),
            pltpu.SemaphoreType.DMA((cols_of,)),
            pltpu.SemaphoreType.DMA((2, cols_of)),
            pltpu.SemaphoreType.DMA((2,)),
            pltpu.SemaphoreType.DMA((2,)),
        ],
        compiler_params=pltpu.CompilerParams(collective_id=0, has_side_effects=True),
    )(pix, up)


def sum_kernel(rows_of, count, *refs):
    ins, outs, held = refs[:count], refs[count : 2 * count], refs[2 * count : 3 * count]
    sends, recvs = refs[3 * count :]
    row, col = lax.axis_index("row"), lax.axis_index("col")
    barrier = pltpu.get_barrier_semaphore()
    for k in range(1, rows_of):
        pl.semaphore_signal(
            barrier, inc=1, device_id=(lax.rem(row + k, rows_of), col), device_id_type=MESH
        )
    pl.semaphore_wait(barrier, rows_of - 1)
    copies = []
    for k in range(1, rows_of):
        for n in range(count):
            copy = pltpu.make_async_remote_copy(
                src_ref=ins[n],
                dst_ref=held[n].at[row],
                send_sem=sends.at[n, k - 1],
                recv_sem=recvs.at[n, k - 1],
                device_id=(lax.rem(row + k, rows_of), col),
                device_id_type=MESH,
            )
            copy.start()
            copies.append(copy)
    for n in range(count):
        held[n][row] = ins[n][...]
    for copy in copies:
        copy.wait()
    for n in range(count):
        total = held[n][0].astype(F32)
        for k in range(1, rows_of):
            total = total + held[n][k].astype(F32)
        outs[n][...] = total


def row_sum_kernel(*parts):
    rows_of, count = lax.axis_size("row"), len(parts)
    return pl.pallas_call(
        functools.partial(sum_kernel, rows_of, count),
        out_shape=tuple(jax.ShapeDtypeStruct(part.shape, F32) for part in parts),
        in_specs=[VMEM] * count,
        out_specs=(VMEM,) * count,
        scratch_shapes=[pltpu.VMEM((rows_of,) + part.shape, BF) for part in parts]
        + [pltpu.SemaphoreType.DMA((count, rows_of - 1))] * 2,
        compiler_params=pltpu.CompilerParams(collective_id=1, has_side_effects=True),
    )(*parts)


def spread(field_ref, first, count, taps):
    _, cols, chans = field_ref.shape

    def one(r, carry):
        line = field_ref[first + r]
        wide = line.astype(F32)
        place = lax.broadcasted_iota(jnp.int32, (cols, chans), 0)
        before = jnp.where(place == 0, 0.0, pltpu.roll(wide, 1, 0)).astype(BF)
        after = jnp.where(place == cols - 1, 0.0, pltpu.roll(wide, cols - 1, 0)).astype(BF)
        taps[r] = jnp.concatenate([before, line, after], axis=1)
        return carry

    lax.fori_loop(0, count, one, 0)


def conv_kernel(halo, span, pre_from, backward, field_ref, kernel_ref, *refs):
    pre_ref, act_ref, taps = refs
    tall, cols, chans = field_ref.shape
    rows = tall - 2
    outs = kernel_ref.shape[2]
    step = 2
    spread(field_ref, 0, tall, taps)
    base = lax.axis_index("row") * (rows - 2 * halo) - halo

    def one(n, carry):
        r = n * step
        total = jnp.zeros((step * cols, outs), F32)
        for p in range(3):
            total = total + jnp.dot(
                taps[pl.ds(r + p, step)].reshape(step * cols, 3 * chans),
                kernel_ref[p],
                preferred_element_type=F32,
            )
        total = total.reshape(step, cols, outs)
        line = base + r + lax.broadcasted_iota(jnp.int32, (step, cols, outs), 0)
        inside = (line >= 0) & (line < span)
        if backward:
            pre = pre_ref[pl.ds(pre_from + r, step)]
            logistic = 1.0 / (1.0 + jnp.exp(-pre))
            value = total * (logistic * (1.0 + pre * (1.0 - logistic)))
        else:
            pre_ref[pl.ds(r, step)] = total
            value = total / (1.0 + jnp.exp(-total))
        act_ref[pl.ds(r, step)] = jnp.where(inside, value, 0.0).astype(BF)
        return carry

    lax.fori_loop(0, rows // step, one, 0)


def conv_call(field, kernel, halo, span, pre=None):
    tall, cols, chans = field.shape
    rows, outs = tall - 2, kernel.shape[3]
    backward = pre is not None
    pre_from = (pre.shape[0] - rows) // 2 if backward else 0
    shape = (rows, cols, outs)
    act = jax.ShapeDtypeStruct(shape, BF)
    ops = (field, kernel.reshape(3, 3 * chans, outs)) + ((pre,) if backward else ())
    return pl.pallas_call(
        functools.partial(conv_kernel, halo, span, pre_from, backward),
        out_shape=act if backward else (jax.ShapeDtypeStruct(shape, F32), act),
        in_specs=[VMEM] * len(ops),
        out_specs=VMEM if backward else (VMEM, VMEM),
        scratch_shapes=[pltpu.VMEM((tall, cols, 3 * chans), BF)],
        compiler_params=pltpu.CompilerParams(vmem_limit_bytes=48 * 1024 * 1024),
        cost_estimate=pl.CostEstimate(
            flops=18 * rows * cols * chans * outs, bytes_accessed=4 * rows * cols * outs, transcendentals=0
        ),
    )(*ops)


def grad_kernel(scale, field_from, delta_from, rows, field_ref, delta_ref, out_ref, taps):
    _, cols, chans = field_ref.shape
    outs = delta_ref.shape[2]
    spread(field_ref, field_from, rows + 2, taps)
    delta = delta_ref[delta_from : delta_from + rows].reshape(rows * cols, outs)
    for p in range(3):
        part = lax.dot_general(
            delta,
            taps[p : p + rows].reshape(rows * cols, 3 * chans),
            (((0,), (0,)), ((), ())),
            preferred_element_type=F32,
        )
        out_ref[p] = (part * scale).astype(BF)


def kernel_grad(field, delta, scale, rows):
    chans = field.shape[2]
    field_from, delta_from = (field.shape[0] - rows - 2) // 2, (delta.shape[0] - rows) // 2
    return pl.pallas_call(
        functools.partial(grad_kernel, scale, field_from, delta_from, rows),
        out_shape=jax.ShapeDtypeStruct((3, delta.shape[2], 3 * chans), BF),
        in_specs=[VMEM] * 2,
        out_specs=VMEM,
        scratch_shapes=[pltpu.VMEM((rows + 2, field.shape[1], 3 * chans), BF)],
        compiler_params=pltpu.CompilerParams(vmem_limit_bytes=48 * 1024 * 1024),
        cost_estimate=pl.CostEstimate(
            flops=18 * rows * field.shape[1] * chans * delta.shape[2], bytes_accessed=4 * delta.size, transcendentals=0
        ),
    )(field, delta)


def col_gather(block):
    return lax.all_gather(block, "col", axis=0)


def taps_last(part):
    chans = part.shape[2] // 3
    split = jnp.stack([part[:, :, q * chans : (q + 1) * chans] for q in range(3)], axis=1)
    return split.transpose(2, 3, 0, 1)


def forward_kernel(kernel):
    return kernel.transpose(2, 3, 1, 0)


def back_kernel(kernel):
    return jnp.flip(kernel, (2, 3)).transpose(2, 3, 0, 1)


def per_device(
    pixels, stem_weight, first_weight, second_weight, entry_weight, final_weight, upstream
):
    chans, pix_rows, pix_cols = pixels.shape
    rows, tile_cols = pix_rows // 2, pix_cols // 2
    row_count = lax.axis_size("row")
    col_count = lax.axis_size("col")
    cols = tile_cols * col_count
    group = upstream.shape[0]
    tail = group * col_count
    feats = stem_weight.shape[0]
    norm_scale = 1.0 / math.sqrt(rows * row_count * cols)
    base = lax.axis_index("row") * rows

    def inside(halo):
        pos = base - halo + jnp.arange(rows + 2 * halo)
        return ((pos >= 0) & (pos < rows * row_count))[:, None, None]

    def act(pre, halo):
        return jnp.where(inside(halo), jax.nn.silu(pre), 0.0).astype(BF)

    split = pixels.astype(BF).reshape(chans, pix_rows, tile_cols, 2)
    split = split.transpose(1, 0, 3, 2).reshape(pix_rows, chans * 2 * tile_cols)
    pix, up_own = start(split, upstream.transpose(1, 0, 2))
    order = lax.rem(lax.axis_index("col") - jnp.arange(col_count) + col_count, col_count)
    pix = jnp.take(pix[:, 3 : pix_rows + 2 * RIM - 3], order, axis=0)
    pix = pix.reshape(col_count, pix_rows + 26, chans, 2, tile_cols)
    pix = pix.transpose(2, 3, 1, 0, 4).reshape(chans, 2, pix_rows + 26, cols)
    weights = jnp.concatenate(
        [entry_weight.transpose(2, 3, 0, 1), final_weight.transpose(2, 3, 0, 1)], axis=3
    )
    weights = col_gather(weights).transpose(1, 2, 0, 3, 4).reshape(3, 3, tail, feats + tail)
    entry_all = weights[..., :feats].transpose(2, 3, 0, 1)
    final_all = weights[..., feats:].transpose(2, 3, 0, 1)
    up_all = col_gather(up_own)

    by_row = pix.reshape(chans, 2, rows + 13, 2, cols)
    padded = jnp.pad(by_row, ((0, 0),) * 4 + ((1, 1),))
    stem_rows = rows + 12
    taps = []
    for p in range(4):
        for q in range(4):
            odd, off = ((1, 0), (0, 1), (1, 1), (0, 2))[q]
            taps.append(
                padded[:, odd, p // 2 : p // 2 + stem_rows, p % 2, off : off + cols]
            )
    taps = jnp.stack(taps, axis=1).reshape(chans * 16, stem_rows, cols)
    stem_pre = lax.dot_general(
        taps.reshape(chans * 16, stem_rows * cols),
        stem_weight.reshape(feats, chans * 16),
        (((0,), (1,)), ((), ())),
        preferred_element_type=F32,
    ).reshape(stem_rows, cols, feats)
    stem_act = act(stem_pre, 6)
    span = rows * row_count
    first_pre, first_act = conv_call(stem_act, forward_kernel(first_weight), 5, span)
    second_pre, second_act = conv_call(first_act, forward_kernel(second_weight), 4, span)
    entry_pre, entry_act = conv_call(second_act, forward_kernel(entry_all), 3, span)

    final_part = kernel_grad(up_own.transpose(0, 2, 1), entry_act, norm_scale, rows)
    up_all = up_all.transpose(1, 3, 0, 2).reshape(rows + 2 * UP_RIM, cols, tail)

    entry_delta = conv_call(up_all, back_kernel(final_all), 3, span, entry_pre)
    own_delta = lax.dynamic_slice_in_dim(
        entry_delta, lax.axis_index("col") * group, group, axis=2
    )
    entry_part = kernel_grad(second_act, own_delta, norm_scale, rows)
    second_delta = conv_call(entry_delta, back_kernel(entry_all), 2, span, second_pre)
    second_part = kernel_grad(first_act, second_delta, norm_scale, rows)
    first_delta = conv_call(second_delta, back_kernel(second_weight), 1, span, first_pre)
    first_part = kernel_grad(stem_act, first_delta, norm_scale, rows)
    stem_delta = conv_call(first_delta, back_kernel(first_weight), 0, span, stem_pre)
    stem_part = lax.dot_general(
        stem_delta.reshape(rows * cols, feats),
        taps[:, 6:-6].reshape(chans * 16, rows * cols),
        (((0,), (1,)), ((), ())),
        preferred_element_type=F32,
    )
    stem_part = (stem_part * norm_scale).astype(BF)
    final_sum, stem_grad, first_grad, second_grad, entry_grad = row_sum_kernel(
        final_part, stem_part, first_part, second_part, entry_part
    )
    final_grad = jnp.flip(taps_last(final_sum), (2, 3)).transpose(1, 0, 2, 3)
    return (
        stem_grad.reshape(stem_weight.shape),
        taps_last(first_grad),
        taps_last(second_grad),
        taps_last(entry_grad),
        final_grad,
    )


def solution(mesh):
    return jax.shard_map(
        per_device,
        mesh=mesh,
        in_specs=(
            P(None, "row", "col"),
            P(),
            P(),
            P(),
            P("col", None, None, None),
            P("col", None, None, None),
            P("col", "row", None),
        ),
        out_specs=(P(), P(), P(), P("col", None, None, None), P("col", None, None, None)),
        check_vma=False,
    )
```

```python
import functools
import math

import jax
import jax.numpy as jnp
from jax import lax
from jax.experimental import pallas as pl
from jax.experimental.pallas import tpu as pltpu
from jax.sharding import PartitionSpec as P

BF = jnp.bfloat16
F32 = jnp.float32


MESH = pl.DeviceIdType.MESH
VMEM = pl.BlockSpec(memory_space=pltpu.VMEM)
RIM = 16
UP_RIM = 4
UNROLL = 2


def start_kernel(rows_of, cols_of, pix_ref, up_ref, pix_out, up_out, sends, pix_recv, rim_recv, up_recv, own_sems):
    row, col = lax.axis_index("row"), lax.axis_index("col")
    tall, up_rows = pix_ref.shape[0], up_ref.shape[0]
    barrier = pltpu.get_barrier_semaphore()
    not_first, not_last = row > 0, row < rows_of - 1

    for k in range(1, cols_of):
        peer = lax.rem(col + k, cols_of)
        pl.semaphore_signal(barrier, inc=1, device_id=(row, peer), device_id_type=MESH)
    for side, there in ((-1, not_first), (1, not_last)):

        @pl.when(there)
        def _():
            for k in range(cols_of):
                peer = lax.rem(col + k, cols_of)
                pl.semaphore_signal(
                    barrier, inc=1, device_id=(row + side, peer), device_id_type=MESH
                )

    bands = 1 + not_first.astype(jnp.int32) + not_last.astype(jnp.int32)
    pl.semaphore_wait(barrier, bands * cols_of - 1)

    def tile_copy(k):
        return pltpu.make_async_remote_copy(
            src_ref=pix_ref,
            dst_ref=pix_out.at[k, RIM : RIM + tall],
            send_sem=sends.at[0, k],
            recv_sem=pix_recv.at[k],
            device_id=(row, lax.rem(col + k, cols_of)),
            device_id_type=MESH,
        )

    def rim_copy(side, k):
        src = pix_ref.at[0:RIM] if side < 0 else pix_ref.at[tall - RIM : tall]
        dst = pix_out.at[k, RIM + tall : tall + 2 * RIM] if side < 0 else pix_out.at[k, 0:RIM]
        at = 0 if side < 0 else 1
        return pltpu.make_async_remote_copy(
            src_ref=src,
            dst_ref=dst,
            send_sem=sends.at[1 + at, k],
            recv_sem=rim_recv.at[at, k],
            device_id=(row + side, lax.rem(col + k, cols_of)),
            device_id_type=MESH,
        )

    def up_copy(side):
        src = up_ref.at[0:UP_RIM] if side < 0 else up_ref.at[up_rows - UP_RIM : up_rows]
        dst = up_out.at[UP_RIM + up_rows : up_rows + 2 * UP_RIM] if side < 0 else up_out.at[0:UP_RIM]
        at = 0 if side < 0 else 1
        return pltpu.make_async_remote_copy(
            src_ref=src,
            dst_ref=dst,
            send_sem=sends.at[3, at],
            recv_sem=up_recv.at[at],
            device_id=(row + side, col),
            device_id_type=MESH,
        )

    sides = ((-1, not_first), (1, not_last))
    for side, there in sides:

        @pl.when(there)
        def _():
            up_copy(side).start()
            for k in range(cols_of):
                rim_copy(side, k).start()

    for k in range(1, cols_of):
        tile_copy(k).start()
    own_pix = pltpu.make_async_copy(pix_ref, pix_out.at[0, RIM : RIM + tall], own_sems.at[0])
    own_up = pltpu.make_async_copy(up_ref, up_out.at[UP_RIM : UP_RIM + up_rows], own_sems.at[1])
    own_pix.start()
    own_up.start()

    @pl.when(row == 0)
    def _():
        for k in range(cols_of):
            pix_out[k, 0:RIM] = jnp.zeros((RIM, pix_ref.shape[1]), BF)
        up_out[0:UP_RIM] = jnp.zeros((UP_RIM,) + up_ref.shape[1:], BF)

    @pl.when(row == rows_of - 1)
    def _():
        for k in range(cols_of):
            pix_out[k, RIM + tall : tall + 2 * RIM] = jnp.zeros((RIM, pix_ref.shape[1]), BF)
        up_out[UP_RIM + up_rows : up_rows + 2 * UP_RIM] = jnp.zeros((UP_RIM,) + up_ref.shape[1:], BF)

    own_pix.wait()
    own_up.wait()
    for k in range(1, cols_of):
        tile_copy(k).wait()
    for side, there in sides:

        @pl.when(there)
        def _():
            up_copy(side).wait_send()
            for k in range(cols_of):
                rim_copy(side, k).wait_send()

        other = not_last if side < 0 else not_first

        @pl.when(other)
        def _():
            up_copy(side).wait_recv()
            for k in range(cols_of):
                rim_copy(side, k).wait_recv()


def start(pix, up):
    rows_of, cols_of = lax.axis_size("row"), lax.axis_size("col")
    return pl.pallas_call(
        functools.partial(start_kernel, rows_of, cols_of),
        out_shape=(
            jax.ShapeDtypeStruct((cols_of, pix.shape[0] + 2 * RIM, pix.shape[1]), BF),
            jax.ShapeDtypeStruct((up.shape[0] + 2 * UP_RIM,) + up.shape[1:], BF),
        ),
        in_specs=[VMEM] * 2,
        out_specs=(VMEM, VMEM),
        scratch_shapes=[
            pltpu.SemaphoreType.DMA((4, cols_of)),
            pltpu.SemaphoreType.DMA((cols_of,)),
            pltpu.SemaphoreType.DMA((2, cols_of)),
            pltpu.SemaphoreType.DMA((2,)),
            pltpu.SemaphoreType.DMA((2,)),
        ],
        compiler_params=pltpu.CompilerParams(collective_id=0, has_side_effects=True),
    )(pix, up)


def sum_kernel(rows_of, count, *refs):
    ins, outs = refs[:count], refs[count : 2 * count]
    held, mine = refs[2 * count : 3 * count], refs[3 * count : 4 * count]
    sends, recvs = refs[4 * count :]
    row, col = lax.axis_index("row"), lax.axis_index("col")
    barrier = pltpu.get_barrier_semaphore()
    for k in range(1, rows_of):
        pl.semaphore_signal(
            barrier, inc=1, device_id=(lax.rem(row + k, rows_of), col), device_id_type=MESH
        )
    pl.semaphore_wait(barrier, rows_of - 1)

    def copy(stage, n, k):
        peer = lax.rem(row + k, rows_of)
        return pltpu.make_async_remote_copy(
            src_ref=ins[n].at[peer] if stage == 0 else mine[n],
            dst_ref=held[n].at[k - 1] if stage == 0 else outs[n].at[row],
            send_sem=sends.at[stage, n, k - 1],
            recv_sem=recvs.at[stage, n, k - 1],
            device_id=(peer, col),
            device_id_type=MESH,
        )

    for n in range(count):
        for k in range(1, rows_of):
            copy(0, n, k).start()
    for n in range(count):
        total = ins[n][row].astype(F32)
        for k in range(1, rows_of):
            copy(0, n, k).wait_recv()
            total = total + held[n][k - 1].astype(F32)
        mine[n][...] = total.astype(BF)
        outs[n][row] = total.astype(BF)
        for k in range(1, rows_of):
            copy(1, n, k).start()
    for n in range(count):
        for k in range(1, rows_of):
            copy(0, n, k).wait_send()
            copy(1, n, k).wait()


def row_sum_kernel(*parts):
    rows_of, count = lax.axis_size("row"), len(parts)
    cut = [part.reshape(rows_of, -1, part.shape[-1]) for part in parts]
    sums = pl.pallas_call(
        functools.partial(sum_kernel, rows_of, count),
        out_shape=tuple(jax.ShapeDtypeStruct(part.shape, BF) for part in cut),
        in_specs=[VMEM] * count,
        out_specs=(VMEM,) * count,
        scratch_shapes=[pltpu.VMEM((rows_of - 1,) + part.shape[1:], BF) for part in cut]
        + [pltpu.VMEM(part.shape[1:], BF) for part in cut]
        + [pltpu.SemaphoreType.DMA((2, count, rows_of - 1))] * 2,
        compiler_params=pltpu.CompilerParams(collective_id=1, has_side_effects=True),
    )(*cut)
    return [total.reshape(part.shape).astype(F32) for total, part in zip(sums, parts)]


def spread(field_ref, first, count, taps, backward=False):
    cols, chans = taps.shape[1], taps.shape[2] // 3

    def one(r, carry):
        if len(field_ref.shape) == 4:
            groups = [field_ref[g, first + r] for g in range(field_ref.shape[0])]
            wide = jnp.concatenate(groups, axis=0).astype(F32).T
            line = wide.astype(BF)
        else:
            line = field_ref[first + r]
            wide = line.astype(F32)
        place = lax.broadcasted_iota(jnp.int32, (cols, chans), 0)
        before = jnp.where(place == 0, 0.0, pltpu.roll(wide, 1, 0)).astype(BF)
        after = jnp.where(place == cols - 1, 0.0, pltpu.roll(wide, cols - 1, 0)).astype(BF)
        near = [after, line, before] if backward else [before, line, after]
        taps[r] = jnp.concatenate(near, axis=1)
        return carry

    lax.fori_loop(0, count, one, 0, unroll=2)


def conv_kernel(halo, span, pre_from, backward, first, field_ref, kernel_ref, *refs):
    pre_ref, act_ref, taps = refs
    tall, cols, wide = taps.shape
    rows, outs = tall - 2, act_ref.shape[2]
    step = 2
    spread(field_ref, 0, tall, taps, backward)
    base = lax.axis_index("row") * (rows - 2 * halo) - halo

    def one(n, carry):
        r = n * step
        total = jnp.zeros((step * cols, outs), F32)
        for p in range(3):
            total = total + jnp.dot(
                taps[pl.ds(r + p, step)].reshape(step * cols, wide),
                kernel_ref[2 - p if backward else p, :, first : first + outs],
                preferred_element_type=F32,
            )
        total = total.reshape(step, cols, outs)
        line = base + r + lax.broadcasted_iota(jnp.int32, (step, cols, outs), 0)
        inside = (line >= 0) & (line < span)
        if backward:
            pre = pre_ref[pl.ds(pre_from + r, step)]
            logistic = 1.0 / (1.0 + jnp.exp(-pre))
            value = total * (logistic * (1.0 + pre * (1.0 - logistic)))
        else:
            pre_ref[pl.ds(r, step)] = total
            value = total / (1.0 + jnp.exp(-total))
        act_ref[pl.ds(r, step)] = jnp.where(inside, value, 0.0).astype(BF)
        return carry

    lax.fori_loop(0, rows // step, one, 0, unroll=UNROLL)


def conv_call(field, kernel, halo, span, pre=None, first=0, outs=None):
    if field.ndim == 4:
        tall, cols, chans = field.shape[1], field.shape[3], field.shape[0] * field.shape[2]
    else:
        tall, cols, chans = field.shape
    rows, outs = tall - 2, outs or kernel.shape[3]
    backward = pre is not None
    pre_from = (pre.shape[0] - rows) // 2 if backward else 0
    shape = (rows, cols, outs)
    act = jax.ShapeDtypeStruct(shape, BF)
    ops = (field, kernel.reshape(3, 3 * chans, kernel.shape[3])) + ((pre,) if backward else ())
    return pl.pallas_call(
        functools.partial(conv_kernel, halo, span, pre_from, backward, first),
        out_shape=act if backward else (jax.ShapeDtypeStruct(shape, F32), act),
        in_specs=[VMEM] * len(ops),
        out_specs=VMEM if backward else (VMEM, VMEM),
        scratch_shapes=[pltpu.VMEM((tall, cols, 3 * chans), BF)],
        compiler_params=pltpu.CompilerParams(vmem_limit_bytes=48 * 1024 * 1024),
        cost_estimate=pl.CostEstimate(
            flops=18 * rows * cols * chans * outs, bytes_accessed=4 * rows * cols * outs, transcendentals=0
        ),
    )(*ops)


def grad_kernel(scale, field_from, delta_from, rows, field_ref, delta_ref, out_ref, taps):
    _, cols, chans = field_ref.shape
    outs = delta_ref.shape[2]
    spread(field_ref, field_from, rows + 2, taps)
    delta = delta_ref[delta_from : delta_from + rows].reshape(rows * cols, outs)
    for p in range(3):
        part = lax.dot_general(
            delta,
            taps[p : p + rows].reshape(rows * cols, 3 * chans),
            (((0,), (0,)), ((), ())),
            preferred_element_type=F32,
        )
        out_ref[p] = (part * scale).astype(BF)


def kernel_grad(field, delta, scale, rows):
    chans = field.shape[2]
    field_from, delta_from = (field.shape[0] - rows - 2) // 2, (delta.shape[0] - rows) // 2
    return pl.pallas_call(
        functools.partial(grad_kernel, scale, field_from, delta_from, rows),
        out_shape=jax.ShapeDtypeStruct((3, delta.shape[2], 3 * chans), BF),
        in_specs=[VMEM] * 2,
        out_specs=VMEM,
        scratch_shapes=[pltpu.VMEM((rows + 2, field.shape[1], 3 * chans), BF)],
        compiler_params=pltpu.CompilerParams(vmem_limit_bytes=48 * 1024 * 1024),
        cost_estimate=pl.CostEstimate(
            flops=18 * rows * field.shape[1] * chans * delta.shape[2], bytes_accessed=4 * delta.size, transcendentals=0
        ),
    )(field, delta)


def col_gather(block):
    return lax.all_gather(block, "col", axis=0)


def taps_last(part):
    chans = part.shape[2] // 3
    split = jnp.stack([part[:, :, q * chans : (q + 1) * chans] for q in range(3)], axis=1)
    return split.transpose(2, 3, 0, 1)


def forward_kernel(kernel):
    return kernel.transpose(2, 3, 1, 0)


def back_kernel(kernel):
    return kernel.transpose(2, 3, 0, 1)


def per_device(
    pixels, stem_weight, first_weight, second_weight, entry_weight, final_weight, upstream
):
    chans, pix_rows, pix_cols = pixels.shape
    rows, tile_cols = pix_rows // 2, pix_cols // 2
    row_count = lax.axis_size("row")
    col_count = lax.axis_size("col")
    cols = tile_cols * col_count
    group = upstream.shape[0]
    tail = group * col_count
    feats = stem_weight.shape[0]
    norm_scale = 1.0 / math.sqrt(rows * row_count * cols)
    base = lax.axis_index("row") * rows

    def inside(halo):
        pos = base - halo + jnp.arange(rows + 2 * halo)
        return ((pos >= 0) & (pos < rows * row_count))[:, None, None]

    def act(pre, halo):
        return jnp.where(inside(halo), jax.nn.silu(pre), 0.0).astype(BF)

    split = pixels.astype(BF).reshape(chans, pix_rows, tile_cols, 2)
    split = split.transpose(1, 0, 3, 2).reshape(pix_rows, chans * 2 * tile_cols)
    pix, up_own = start(split, upstream.transpose(1, 0, 2))
    order = lax.rem(lax.axis_index("col") - jnp.arange(col_count) + col_count, col_count)
    pix = jnp.take(pix[:, 3 : pix_rows + 2 * RIM - 3], order, axis=0)
    pix = pix.reshape(col_count, pix_rows + 26, chans, 2, tile_cols)
    pix = pix.transpose(2, 3, 1, 0, 4).reshape(chans, 2, pix_rows + 26, cols)
    weights = jnp.concatenate([back_kernel(final_weight), back_kernel(entry_weight)], axis=3)
    weights = col_gather(weights).transpose(1, 2, 0, 3, 4).reshape(3, 3, tail, tail + feats)
    entry_forward = weights[..., tail:].transpose(0, 1, 3, 2)
    up_all = col_gather(up_own)

    by_row = pix.reshape(chans, 2, rows + 13, 2, cols)
    padded = jnp.pad(by_row, ((0, 0),) * 4 + ((1, 1),))
    stem_rows = rows + 12
    taps = []
    for p in range(4):
        for q in range(4):
            odd, off = ((1, 0), (0, 1), (1, 1), (0, 2))[q]
            taps.append(
                padded[:, odd, p // 2 : p // 2 + stem_rows, p % 2, off : off + cols]
            )
    taps = jnp.stack(taps, axis=1).reshape(chans * 16, stem_rows, cols)
    stem_pre = lax.dot_general(
        taps.reshape(chans * 16, stem_rows * cols),
        stem_weight.reshape(feats, chans * 16),
        (((0,), (1,)), ((), ())),
        preferred_element_type=F32,
    ).reshape(stem_rows, cols, feats)
    stem_act = act(stem_pre, 6)
    span = rows * row_count
    first_pre, first_act = conv_call(stem_act, forward_kernel(first_weight), 5, span)
    second_pre, second_act = conv_call(first_act, forward_kernel(second_weight), 4, span)
    entry_pre, entry_act = conv_call(second_act, entry_forward, 3, span)

    final_part = kernel_grad(up_own.transpose(0, 2, 1), entry_act, norm_scale, rows)
    entry_delta = conv_call(up_all, weights, 3, span, entry_pre, 0, tail)
    own_delta = lax.dynamic_slice_in_dim(
        entry_delta, lax.axis_index("col") * group, group, axis=2
    )
    entry_part = kernel_grad(second_act, own_delta, norm_scale, rows)
    second_delta = conv_call(entry_delta, weights, 2, span, second_pre, tail, feats)
    second_part = kernel_grad(first_act, second_delta, norm_scale, rows)
    first_delta = conv_call(second_delta, back_kernel(second_weight), 1, span, first_pre)
    first_part = kernel_grad(stem_act, first_delta, norm_scale, rows)
    stem_delta = conv_call(first_delta, back_kernel(first_weight), 0, span, stem_pre)
    stem_part = lax.dot_general(
        stem_delta.reshape(rows * cols, feats),
        taps[:, 6:-6].reshape(chans * 16, rows * cols),
        (((0,), (1,)), ((), ())),
        preferred_element_type=F32,
    )
    stem_part = (stem_part * norm_scale).astype(BF)
    final_sum, stem_grad, first_grad, second_grad, entry_grad = row_sum_kernel(
        final_part, stem_part, first_part, second_part, entry_part
    )
    final_grad = jnp.flip(taps_last(final_sum), (2, 3)).transpose(1, 0, 2, 3)
    return (
        stem_grad.reshape(stem_weight.shape),
        taps_last(first_grad),
        taps_last(second_grad),
        taps_last(entry_grad),
        final_grad,
    )


def solution(mesh):
    return jax.shard_map(
        per_device,
        mesh=mesh,
        in_specs=(
            P(None, "row", "col"),
            P(),
            P(),
            P(),
            P("col", None, None, None),
            P("col", None, None, None),
            P("col", "row", None),
        ),
        out_specs=(P(), P(), P(), P("col", None, None, None), P("col", None, None, None)),
        check_vma=False,
    )
```

```python
import functools
import math

import jax
import jax.numpy as jnp
from jax import lax
from jax.experimental import pallas as pl
from jax.experimental.pallas import tpu as pltpu
from jax.sharding import PartitionSpec as P

BF = jnp.bfloat16
F32 = jnp.float32


MESH = pl.DeviceIdType.MESH
VMEM = pl.BlockSpec(memory_space=pltpu.VMEM)
RIM = 16
UP_RIM = 4
UNROLL = 4


def start_kernel(rows_of, cols_of, pix_ref, up_ref, pix_out, up_out, sends, pix_recv, rim_recv, up_recv):
    row, col = lax.axis_index("row"), lax.axis_index("col")
    tall, up_rows = pix_ref.shape[0], up_ref.shape[0]
    barrier = pltpu.get_barrier_semaphore()
    not_first, not_last = row > 0, row < rows_of - 1

    for k in range(1, cols_of):
        peer = lax.rem(col + k, cols_of)
        pl.semaphore_signal(barrier, inc=1, device_id=(row, peer), device_id_type=MESH)
    for side, there in ((-1, not_first), (1, not_last)):

        @pl.when(there)
        def _():
            for k in range(cols_of):
                peer = lax.rem(col + k, cols_of)
                pl.semaphore_signal(
                    barrier, inc=1, device_id=(row + side, peer), device_id_type=MESH
                )

    bands = 1 + not_first.astype(jnp.int32) + not_last.astype(jnp.int32)
    pl.semaphore_wait(barrier, bands * cols_of - 1)

    def tile_copy(k):
        return pltpu.make_async_remote_copy(
            src_ref=pix_ref,
            dst_ref=pix_out.at[k, RIM : RIM + tall],
            send_sem=sends.at[0, k],
            recv_sem=pix_recv.at[k],
            device_id=(row, lax.rem(col + k, cols_of)),
            device_id_type=MESH,
        )

    def rim_copy(side, k):
        src = pix_ref.at[0:RIM] if side < 0 else pix_ref.at[tall - RIM : tall]
        dst = pix_out.at[k, RIM + tall : tall + 2 * RIM] if side < 0 else pix_out.at[k, 0:RIM]
        at = 0 if side < 0 else 1
        return pltpu.make_async_remote_copy(
            src_ref=src,
            dst_ref=dst,
            send_sem=sends.at[1 + at, k],
            recv_sem=rim_recv.at[at, k],
            device_id=(row + side, lax.rem(col + k, cols_of)),
            device_id_type=MESH,
        )

    def up_copy(side):
        src = up_ref.at[0:UP_RIM] if side < 0 else up_ref.at[up_rows - UP_RIM : up_rows]
        dst = up_out.at[UP_RIM + up_rows : up_rows + 2 * UP_RIM] if side < 0 else up_out.at[0:UP_RIM]
        at = 0 if side < 0 else 1
        return pltpu.make_async_remote_copy(
            src_ref=src,
            dst_ref=dst,
            send_sem=sends.at[3, at],
            recv_sem=up_recv.at[at],
            device_id=(row + side, col),
            device_id_type=MESH,
        )

    sides = ((-1, not_first), (1, not_last))
    for side, there in sides:

        @pl.when(there)
        def _():
            up_copy(side).start()
            for k in range(cols_of):
                rim_copy(side, k).start()

    for k in range(1, cols_of):
        tile_copy(k).start()
    pix_out[0, RIM : RIM + tall] = pix_ref[...]
    up_out[UP_RIM : UP_RIM + up_rows] = up_ref[...]

    @pl.when(row == 0)
    def _():
        for k in range(cols_of):
            pix_out[k, 0:RIM] = jnp.zeros((RIM, pix_ref.shape[1]), BF)
        up_out[0:UP_RIM] = jnp.zeros((UP_RIM,) + up_ref.shape[1:], BF)

    @pl.when(row == rows_of - 1)
    def _():
        for k in range(cols_of):
            pix_out[k, RIM + tall : tall + 2 * RIM] = jnp.zeros((RIM, pix_ref.shape[1]), BF)
        up_out[UP_RIM + up_rows : up_rows + 2 * UP_RIM] = jnp.zeros((UP_RIM,) + up_ref.shape[1:], BF)

    for k in range(1, cols_of):
        tile_copy(k).wait()
    for side, there in sides:

        @pl.when(there)
        def _():
            up_copy(side).wait_send()
            for k in range(cols_of):
                rim_copy(side, k).wait_send()

        other = not_last if side < 0 else not_first

        @pl.when(other)
        def _():
            up_copy(side).wait_recv()
            for k in range(cols_of):
                rim_copy(side, k).wait_recv()


def start(pix, up):
    rows_of, cols_of = lax.axis_size("row"), lax.axis_size("col")
    return pl.pallas_call(
        functools.partial(start_kernel, rows_of, cols_of),
        out_shape=(
            jax.ShapeDtypeStruct((cols_of, pix.shape[0] + 2 * RIM, pix.shape[1]), BF),
            jax.ShapeDtypeStruct((up.shape[0] + 2 * UP_RIM,) + up.shape[1:], BF),
        ),
        in_specs=[VMEM] * 2,
        out_specs=(VMEM, VMEM),
        scratch_shapes=[
            pltpu.SemaphoreType.DMA((4, cols_of)),
            pltpu.SemaphoreType.DMA((cols_of,)),
            pltpu.SemaphoreType.DMA((2, cols_of)),
            pltpu.SemaphoreType.DMA((2,)),
        ],
        compiler_params=pltpu.CompilerParams(collective_id=0, has_side_effects=True),
    )(pix, up)


def sum_kernel(rows_of, count, *refs):
    ins, outs = refs[:count], refs[count : 2 * count]
    held, mine = refs[2 * count : 3 * count], refs[3 * count : 4 * count]
    sends, recvs = refs[4 * count :]
    row, col = lax.axis_index("row"), lax.axis_index("col")
    barrier = pltpu.get_barrier_semaphore()
    for k in range(1, rows_of):
        pl.semaphore_signal(
            barrier, inc=1, device_id=(lax.rem(row + k, rows_of), col), device_id_type=MESH
        )
    pl.semaphore_wait(barrier, rows_of - 1)

    def copy(stage, n, k):
        peer = lax.rem(row + k, rows_of)
        return pltpu.make_async_remote_copy(
            src_ref=ins[n].at[peer] if stage == 0 else mine[n],
            dst_ref=held[n].at[k - 1] if stage == 0 else outs[n].at[row],
            send_sem=sends.at[stage, n, k - 1],
            recv_sem=recvs.at[stage, n, k - 1],
            device_id=(peer, col),
            device_id_type=MESH,
        )

    for n in range(count):
        for k in range(1, rows_of):
            copy(0, n, k).start()
    for n in range(count):
        total = ins[n][row].astype(F32)
        for k in range(1, rows_of):
            copy(0, n, k).wait_recv()
            total = total + held[n][k - 1].astype(F32)
        mine[n][...] = total.astype(BF)
        outs[n][row] = total.astype(BF)
        for k in range(1, rows_of):
            copy(1, n, k).start()
    for n in range(count):
        for k in range(1, rows_of):
            copy(0, n, k).wait_send()
            copy(1, n, k).wait()


def row_sum_kernel(*parts):
    rows_of, count = lax.axis_size("row"), len(parts)
    cut = [part.reshape(rows_of, -1, part.shape[-1]) for part in parts]
    sums = pl.pallas_call(
        functools.partial(sum_kernel, rows_of, count),
        out_shape=tuple(jax.ShapeDtypeStruct(part.shape, BF) for part in cut),
        in_specs=[VMEM] * count,
        out_specs=(VMEM,) * count,
        scratch_shapes=[pltpu.VMEM((rows_of - 1,) + part.shape[1:], BF) for part in cut]
        + [pltpu.VMEM(part.shape[1:], BF) for part in cut]
        + [pltpu.SemaphoreType.DMA((2, count, rows_of - 1))] * 2,
        compiler_params=pltpu.CompilerParams(collective_id=1, has_side_effects=True),
    )(*cut)
    return [total.reshape(part.shape).astype(F32) for total, part in zip(sums, parts)]


def spread(field_ref, first, count, taps, backward=False):
    cols, chans = taps.shape[1], taps.shape[2] // 3

    def one(r, carry):
        if len(field_ref.shape) == 4:
            groups = [field_ref[g, first + r] for g in range(field_ref.shape[0])]
            wide = jnp.concatenate(groups, axis=0).astype(F32).T
            line = wide.astype(BF)
        else:
            line = field_ref[first + r]
            wide = line.astype(F32)
        place = lax.broadcasted_iota(jnp.int32, (cols, chans), 0)
        before = jnp.where(place == 0, 0.0, pltpu.roll(wide, 1, 0)).astype(BF)
        after = jnp.where(place == cols - 1, 0.0, pltpu.roll(wide, cols - 1, 0)).astype(BF)
        near = [after, line, before] if backward else [before, line, after]
        taps[r] = jnp.concatenate(near, axis=1)
        return carry

    lax.fori_loop(0, count, one, 0, unroll=2)


def conv_kernel(halo, span, pre_from, backward, first, field_ref, kernel_ref, *refs):
    pre_ref, act_ref, taps = refs
    tall, cols, wide = taps.shape
    rows, outs = tall - 2, act_ref.shape[2]
    step = 2
    spread(field_ref, 0, tall, taps, backward)
    base = lax.axis_index("row") * (rows - 2 * halo) - halo

    def one(n, carry):
        r = n * step
        total = jnp.zeros((step * cols, outs), F32)
        for p in range(3):
            total = total + jnp.dot(
                taps[pl.ds(r + p, step)].reshape(step * cols, wide),
                kernel_ref[2 - p if backward else p, :, first : first + outs],
                preferred_element_type=F32,
            )
        total = total.reshape(step, cols, outs)
        line = base + r + lax.broadcasted_iota(jnp.int32, (step, cols, outs), 0)
        inside = (line >= 0) & (line < span)
        if backward:
            pre = pre_ref[pl.ds(pre_from + r, step)]
            logistic = 1.0 / (1.0 + jnp.exp(-pre))
            value = total * (logistic * (1.0 + pre * (1.0 - logistic)))
        else:
            pre_ref[pl.ds(r, step)] = total
            value = total / (1.0 + jnp.exp(-total))
        act_ref[pl.ds(r, step)] = jnp.where(inside, value, 0.0).astype(BF)
        return carry

    lax.fori_loop(0, rows // step, one, 0, unroll=UNROLL)


def conv_call(field, kernel, halo, span, pre=None, first=0, outs=None):
    if field.ndim == 4:
        tall, cols, chans = field.shape[1], field.shape[3], field.shape[0] * field.shape[2]
    else:
        tall, cols, chans = field.shape
    rows, outs = tall - 2, outs or kernel.shape[3]
    backward = pre is not None
    pre_from = (pre.shape[0] - rows) // 2 if backward else 0
    shape = (rows, cols, outs)
    act = jax.ShapeDtypeStruct(shape, BF)
    ops = (field, kernel.reshape(3, 3 * chans, kernel.shape[3])) + ((pre,) if backward else ())
    return pl.pallas_call(
        functools.partial(conv_kernel, halo, span, pre_from, backward, first),
        out_shape=act if backward else (jax.ShapeDtypeStruct(shape, F32), act),
        in_specs=[VMEM] * len(ops),
        out_specs=VMEM if backward else (VMEM, VMEM),
        scratch_shapes=[pltpu.VMEM((tall, cols, 3 * chans), BF)],
        compiler_params=pltpu.CompilerParams(vmem_limit_bytes=24 * 1024 * 1024),
        cost_estimate=pl.CostEstimate(
            flops=18 * rows * cols * chans * outs, bytes_accessed=4 * rows * cols * outs, transcendentals=0
        ),
    )(*ops)


def grad_kernel(scale, field_from, delta_from, rows, field_ref, delta_ref, out_ref, taps):
    _, cols, chans = field_ref.shape
    outs = delta_ref.shape[2]
    spread(field_ref, field_from, rows + 2, taps)
    delta = delta_ref[delta_from : delta_from + rows].reshape(rows * cols, outs)
    for p in range(3):
        part = lax.dot_general(
            delta,
            taps[p : p + rows].reshape(rows * cols, 3 * chans),
            (((0,), (0,)), ((), ())),
            preferred_element_type=F32,
        )
        out_ref[p] = (part * scale).astype(BF)


def kernel_grad(field, delta, scale, rows):
    chans = field.shape[2]
    field_from, delta_from = (field.shape[0] - rows - 2) // 2, (delta.shape[0] - rows) // 2
    return pl.pallas_call(
        functools.partial(grad_kernel, scale, field_from, delta_from, rows),
        out_shape=jax.ShapeDtypeStruct((3, delta.shape[2], 3 * chans), BF),
        in_specs=[VMEM] * 2,
        out_specs=VMEM,
        scratch_shapes=[pltpu.VMEM((rows + 2, field.shape[1], 3 * chans), BF)],
        compiler_params=pltpu.CompilerParams(vmem_limit_bytes=24 * 1024 * 1024),
        cost_estimate=pl.CostEstimate(
            flops=18 * rows * field.shape[1] * chans * delta.shape[2], bytes_accessed=4 * delta.size, transcendentals=0
        ),
    )(field, delta)


def col_gather(block):
    return lax.all_gather(block, "col", axis=0)


def taps_last(part):
    chans = part.shape[2] // 3
    split = jnp.stack([part[:, :, q * chans : (q + 1) * chans] for q in range(3)], axis=1)
    return split.transpose(2, 3, 0, 1)


def forward_kernel(kernel):
    return kernel.transpose(2, 3, 1, 0)


def back_kernel(kernel):
    return kernel.transpose(2, 3, 0, 1)


def per_device(
    pixels, stem_weight, first_weight, second_weight, entry_weight, final_weight, upstream
):
    chans, pix_rows, pix_cols = pixels.shape
    rows, tile_cols = pix_rows // 2, pix_cols // 2
    row_count = lax.axis_size("row")
    col_count = lax.axis_size("col")
    cols = tile_cols * col_count
    group = upstream.shape[0]
    tail = group * col_count
    feats = stem_weight.shape[0]
    norm_scale = 1.0 / math.sqrt(rows * row_count * cols)
    base = lax.axis_index("row") * rows

    def inside(halo):
        pos = base - halo + jnp.arange(rows + 2 * halo)
        return ((pos >= 0) & (pos < rows * row_count))[:, None, None]

    def act(pre, halo):
        return jnp.where(inside(halo), jax.nn.silu(pre), 0.0).astype(BF)

    split = pixels.astype(BF).reshape(chans, pix_rows, tile_cols, 2)
    split = split.transpose(1, 0, 3, 2).reshape(pix_rows, chans * 2 * tile_cols)
    pix, up_own = start(split, upstream.transpose(1, 0, 2))
    order = lax.rem(lax.axis_index("col") - jnp.arange(col_count) + col_count, col_count)
    pix = jnp.take(pix[:, 3 : pix_rows + 2 * RIM - 3], order, axis=0)
    pix = pix.reshape(col_count, pix_rows + 26, chans, 2, tile_cols)
    pix = pix.transpose(2, 3, 1, 0, 4).reshape(chans, 2, pix_rows + 26, cols)
    weights = jnp.concatenate([back_kernel(final_weight), back_kernel(entry_weight)], axis=3)
    weights = col_gather(weights).transpose(1, 2, 0, 3, 4).reshape(3, 3, tail, tail + feats)
    entry_forward = weights[..., tail:].transpose(0, 1, 3, 2)
    up_all = col_gather(up_own)

    by_row = pix.reshape(chans, 2, rows + 13, 2, cols)
    padded = jnp.pad(by_row, ((0, 0),) * 4 + ((1, 1),))
    stem_rows = rows + 12
    taps = []
    for p in range(4):
        for q in range(4):
            odd, off = ((1, 0), (0, 1), (1, 1), (0, 2))[q]
            taps.append(
                padded[:, odd, p // 2 : p // 2 + stem_rows, p % 2, off : off + cols]
            )
    taps = jnp.stack(taps, axis=1).reshape(chans * 16, stem_rows, cols)
    stem_pre = lax.dot_general(
        taps.reshape(chans * 16, stem_rows * cols),
        stem_weight.reshape(feats, chans * 16),
        (((0,), (1,)), ((), ())),
        preferred_element_type=F32,
    ).reshape(stem_rows, cols, feats)
    stem_act = act(stem_pre, 6)
    span = rows * row_count
    first_pre, first_act = conv_call(stem_act, forward_kernel(first_weight), 5, span)
    second_pre, second_act = conv_call(first_act, forward_kernel(second_weight), 4, span)
    entry_pre, entry_act = conv_call(second_act, entry_forward, 3, span)

    final_part = kernel_grad(up_own.transpose(0, 2, 1), entry_act, norm_scale, rows)
    entry_delta = conv_call(up_all, weights, 3, span, entry_pre, 0, tail)
    own_delta = lax.dynamic_slice_in_dim(
        entry_delta, lax.axis_index("col") * group, group, axis=2
    )
    entry_part = kernel_grad(second_act, own_delta, norm_scale, rows)
    second_delta = conv_call(entry_delta, weights, 2, span, second_pre, tail, feats)
    second_part = kernel_grad(first_act, second_delta, norm_scale, rows)
    first_delta = conv_call(second_delta, back_kernel(second_weight), 1, span, first_pre)
    first_part = kernel_grad(stem_act, first_delta, norm_scale, rows)
    stem_delta = conv_call(first_delta, back_kernel(first_weight), 0, span, stem_pre)
    stem_part = lax.dot_general(
        stem_delta.reshape(rows * cols, feats),
        taps[:, 6:-6].reshape(chans * 16, rows * cols),
        (((0,), (1,)), ((), ())),
        preferred_element_type=F32,
    )
    stem_part = (stem_part * norm_scale).astype(BF)
    final_sum, stem_grad, first_grad, second_grad, entry_grad = row_sum_kernel(
        final_part, stem_part, first_part, second_part, entry_part
    )
    final_grad = jnp.flip(taps_last(final_sum), (2, 3)).transpose(1, 0, 2, 3)
    return (
        stem_grad.reshape(stem_weight.shape),
        taps_last(first_grad),
        taps_last(second_grad),
        taps_last(entry_grad),
        final_grad,
    )


def solution(mesh):
    return jax.shard_map(
        per_device,
        mesh=mesh,
        in_specs=(
            P(None, "row", "col"),
            P(),
            P(),
            P(),
            P("col", None, None, None),
            P("col", None, None, None),
            P("col", "row", None),
        ),
        out_specs=(P(), P(), P(), P("col", None, None, None), P("col", None, None, None)),
        check_vma=False,
    )
```
